256 devices in a mesh: band: 4 (over x), row: 4 (over y_hi, core), col: 16 (over y_lo, z).
Axes of the slice: x: 4, y: 4 (y_hi: 2, y_lo: 2; y = y_hi * 2 + y_lo), z: 8, core: 2. Of those that a mesh axis runs over, the one named last changes fastest.
Arguments:
- tokens: bfloat16 [256, 32, 16, 1024], P(('band', 'row'), 'col'), may hold values from -10 to 10
- counts: int32 [4], replicated, may hold values from 1 to 4, as said below
- norm_band: bfloat16 [1024], replicated, may hold values from 0.099609375 to 1.8984375
- w_band_qkv: bfloat16 [1024, 1536], replicated, may hold values from -1 to 1
- w_band_out: bfloat16 [512, 1024], replicated, may hold values from -0.25 to 0.25
- norm_space: bfloat16 [1024], replicated, may hold values from 0.099609375 to 1.8984375
- w_space_qkv: bfloat16 [1024, 1536], replicated, may hold values from -1 to 1
- w_space_out: bfloat16 [512, 1024], replicated, may hold values from -0.25 to 0.25
Outputs:
- layer_out: bfloat16 [256, 32, 16, 1024], P(('band', 'row'), 'col')
The draws below stay inside these ranges and needn't reach their ends.
Inputs may be any that keep to these rules, and one draw needn't show every extreme that they name: `counts`: every group holds at least one live token; some group is full and some group holds exactly one.
All inputs are finite; a program needn't handle non-finite values.
Results may differ from the reference program's by a relative error of at most 0.0063.
Values may be sent and summed in bfloat16 or wider, within the bound.
No kernel may reach another device: no remote copies, remote signals or barrier semaphores. Data moves between devices by JAX's collectives and lax.ppermute only.
A program may use at most 128 MiB of HBM per device.

```python
import math
import jax
import jax.numpy as jnp
from jax import lax

D = 1024
HD = 64
HB = 8
HR = 4
HC = 4
BGROUPS = 4
BCAP = 4
NR = 256
NC = 32
BS = 16


def draw_tokens(key, part):
    base = jax.random.normal(jax.random.fold_in(key, 1), (NR, NC, BS, D), jnp.float32)
    return jnp.clip(base, -10.0, 10.0).astype(jnp.bfloat16)


def spiked_weight(key, salt, heads):
    weights = jax.random.normal(jax.random.fold_in(key, salt), (D, 3 * heads * HD), jnp.float32) / math.sqrt(D)
    return jnp.clip(weights, -1.0, 1.0)


def draw_w_band_qkv(key, part):
    return spiked_weight(key, 11, HB).astype(jnp.bfloat16)


def draw_w_space_qkv(key, part):
    return spiked_weight(key, 21, HR + HC).astype(jnp.bfloat16)


def draw_counts(key, part):
    drawn = jax.random.randint(jax.random.fold_in(key, 5), (BGROUPS,), 1, BCAP + 1)
    fullest = jax.random.randint(jax.random.fold_in(key, 6), (), 0, BGROUPS)
    offset = jax.random.randint(jax.random.fold_in(key, 7), (), 1, BGROUPS)
    sparsest = (fullest + offset) % BGROUPS
    groups = jnp.arange(BGROUPS)
    drawn = jnp.where(groups == sparsest, 1, drawn)
    return jnp.where(groups == fullest, BCAP, drawn).astype(jnp.int32)


def noise(key, dims, spread, limit, kind=jnp.bfloat16):
    result = spread * jax.random.normal(key, dims, jnp.float32)
    return jnp.clip(result, min=-limit, max=limit).astype(kind)


def setup_inputs(seed: int = 0) -> dict:
    splits = jax.random.split(jax.random.key(seed), 9)
    return {
        "tokens": draw_tokens(jax.random.fold_in(splits[8], 71), 0),
        "counts": draw_counts(jax.random.fold_in(splits[8], 71), 0),
        "norm_band": jnp.clip(1.0 + 0.18 * jax.random.normal(splits[2], (D,), jnp.float32), 0.099609375, 1.8984375).astype(jnp.bfloat16),
        "w_band_qkv": draw_w_band_qkv(jax.random.fold_in(splits[8], 71), 0),
        "w_band_out": noise(splits[4], (HB * HD, D), (HB * HD) ** -0.5, 0.25),
        "norm_space": jnp.clip(1.0 + 0.18 * jax.random.normal(splits[5], (D,), jnp.float32), 0.099609375, 1.8984375).astype(jnp.bfloat16),
        "w_space_qkv": draw_w_space_qkv(jax.random.fold_in(splits[8], 71), 0),
        "w_space_out": noise(splits[7], ((HR + HC) * HD, D), ((HR + HC) * HD) ** -0.5, 0.25),
    }


EPS = 1e-06

def rms_norm(values, gain):
    wide = values.astype(jnp.float32)
    scale = lax.rsqrt(lax.optimization_barrier(jnp.mean(wide * wide, axis=-1, keepdims=True)) + EPS)
    return (wide * scale * gain.astype(jnp.float32)).astype(jnp.bfloat16)

def widen(values):
    return lax.optimization_barrier(values.astype(jnp.bfloat16)).astype(jnp.float32)

def band_rows(token_row, live, norm_band, w_band_qkv, w_band_out, norm_space, w_space_qkv):
    normed = rms_norm(token_row, norm_band)
    qkv = widen(jnp.dot(normed.reshape(-1, D), w_band_qkv, preferred_element_type=jnp.float32))
    qkv = qkv.reshape(NC, BS, 3, HB, HD)
    scores = jnp.einsum('pihd,pjhd->phij', qkv[:, :, 0], qkv[:, :, 1]) * HD ** (-0.5)
    scores = jnp.where(live[None, None, None, :], scores, -1e+30)
    top = lax.optimization_barrier(jnp.max(scores, axis=-1, keepdims=True))
    probs = jnp.exp(scores - top)
    total = lax.optimization_barrier(jnp.sum(probs, axis=-1))
    mixed = jnp.einsum('phij,pjhd->pihd', widen(probs), qkv[:, :, 2])
    mixed = mixed / jnp.transpose(total, (0, 2, 1))[..., None]
    heads_out = mixed.astype(jnp.bfloat16).reshape(NC * BS, HB * HD)
    resid = token_row.astype(jnp.float32) + jnp.dot(heads_out, w_band_out, preferred_element_type=jnp.float32).reshape(NC, BS, D)
    normed2 = rms_norm(resid, norm_space)
    space_qkv = jnp.dot(normed2.reshape(-1, D), w_space_qkv, preferred_element_type=jnp.float32).astype(jnp.bfloat16)
    return (resid, space_qkv.reshape(NC, BS, 3, HR + HC, HD))

def axial(block, first, last):
    query = widen(block[:, :, 0, first:last])
    keys = widen(block[:, :, 1, first:last])
    vals = widen(block[:, :, 2, first:last])
    scores = jnp.einsum('ishd,jshd->shij', query, keys) * HD ** (-0.5)
    top = lax.optimization_barrier(jnp.max(scores, axis=-1, keepdims=True))
    probs = jnp.exp(scores - top)
    total = lax.optimization_barrier(jnp.sum(probs, axis=-1))
    mixed = jnp.einsum('shij,jshd->ishd', widen(probs), vals)
    mixed = mixed / jnp.transpose(total, (2, 0, 1))[..., None]
    return mixed.astype(jnp.bfloat16)

def reference(tokens, counts, norm_band, w_band_qkv, w_band_out, norm_space, w_space_qkv, w_space_out):
    slots = jnp.arange(BS, dtype=jnp.int32)
    live = slots % BCAP < counts[slots // BCAP]
    resid, space_qkv = lax.map(lambda token_row: band_rows(token_row, live, norm_band, w_band_qkv, w_band_out, norm_space, w_space_qkv), tokens)
    row_heads = lax.map(lambda block: axial(block, 0, HR), space_qkv)
    col_heads = lax.map(lambda block: axial(block, HR, HR + HC), jnp.swapaxes(space_qkv, 0, 1))
    col_heads = jnp.swapaxes(col_heads, 0, 1)
    heads = jnp.concatenate([row_heads.reshape(NR, NC, BS, HR * HD), col_heads.reshape(NR, NC, BS, HC * HD)], axis=-1)

    def finish(pair):
        resid_row, heads_row = pair
        mixed = jnp.dot(heads_row.reshape(NC * BS, (HR + HC) * HD), w_space_out, preferred_element_type=jnp.float32)
        return (resid_row + mixed.reshape(NC, BS, D)).astype(jnp.bfloat16)
    return lax.map(finish, (resid, heads))
```

```python
import functools

import jax
import jax.numpy as jnp
from jax import lax
from jax.experimental import pallas as pl
from jax.experimental.pallas import tpu as pltpu
from jax.sharding import PartitionSpec as P

HD = 64
HB = 8
HR = 4
HC = 4
EPS = 1e-06
NEG = -1e30
LOG2E = 1.4426950408889634
SCALE2 = HD**-0.5 * LOG2E
F32 = jnp.float32
BF16 = jnp.bfloat16

VMEM = pl.BlockSpec(memory_space=pltpu.VMEM)
SMEM = pl.BlockSpec(memory_space=pltpu.SMEM)
ANY = pl.BlockSpec(memory_space=pl.ANY)


def dot(a, b):
    return jnp.dot(a, b, preferred_element_type=F32)


def dot_t(a, b):
    return lax.dot_general(a, b, (((1,), (1,)), ((), ())), preferred_element_type=F32)


def halves(pair):
    low = lax.broadcasted_iota(jnp.int32, pair.shape, 1) < HD
    zero = jnp.zeros_like(pair)
    return jnp.concatenate([jnp.where(low, pair, zero), jnp.where(low, zero, pair)], axis=0)


def pair_attention(query, keys2, vals2, mask):
    m = query.shape[0]
    n = keys2.shape[0] // 2
    scores = dot_t(query, keys2)
    probs, totals = [], []
    for h in range(2):
        s = scores[:, h * n : (h + 1) * n]
        if mask is not None:
            s = jnp.where(mask, s, NEG)
        p = jnp.exp2((s - jnp.max(s, axis=-1, keepdims=True)) * SCALE2)
        totals.append(jnp.sum(p, axis=-1, keepdims=True))
        probs.append(p.astype(BF16))
    mixed = dot(jnp.concatenate(probs, axis=1), vals2)
    low = lax.broadcasted_iota(jnp.int32, (m, 2 * HD), 1) < HD
    return (mixed / jnp.where(low, totals[0], totals[1])).astype(BF16)


def rms(x, gain):
    scale = lax.rsqrt(jnp.mean(x * x, axis=-1, keepdims=True) + EPS)
    return (x * scale * gain).astype(BF16)


def local_kernel(
    counts, x_ref, g1_ref, g2_ref, w1_hbm, w2_hbm, w3_hbm,
    resid_ref, row_ref, col_ref,
    w1, w2, w3, normed, qkv, heads, wide, sems,
):
    tokens, width = x_ref.shape
    prows, _, _ = row_ref.shape
    slots = col_ref.shape[0]
    pcols = tokens // prows // slots
    inner = HB * HD
    copies = []
    for i in range(3):
        cols = pl.ds(i * inner, inner)
        copies.append(pltpu.make_async_copy(w1_hbm.at[:, cols], w1.at[:, cols], sems.at[i]))
    copies.append(pltpu.make_async_copy(w2_hbm, w2, sems.at[3]))
    for i in range(3):
        cols = pl.ds(i * inner, inner)
        copies.append(pltpu.make_async_copy(w3_hbm.at[:, cols], w3.at[:, cols], sems.at[4 + i]))
    for c in copies:
        c.start()

    g1 = g1_ref[...].astype(F32)
    for b in range(tokens // 64):
        rows = pl.ds(b * 64, 64)
        normed[rows, :] = rms(x_ref[rows, :].astype(F32), g1)
    for i in range(3):
        copies[i].wait()
        for t in range(inner // 256):
            cols = pl.ds(i * inner + t * 256, 256)
            qkv[:, cols] = dot(normed[...], w1[:, cols]).astype(BF16)

    block = 128
    rowi = lax.broadcasted_iota(jnp.int32, (block, block), 0)
    coli = lax.broadcasted_iota(jnp.int32, (block, block), 1)
    slot = coli % slots
    ngroups = counts.shape[0]
    cap = slots // ngroups
    count = jnp.zeros((block, block), jnp.int32)
    for g in range(ngroups):
        count = jnp.where(slot // cap == g, counts[g], count)
    mask = (rowi // slots == coli // slots) & (slot % cap < count)
    for b in range(tokens // block):
        rows = pl.ds(b * block, block)
        for t in range(HB // 2):
            q = qkv[rows, pl.ds(t * 128, 128)]
            k = qkv[rows, pl.ds(inner + t * 128, 128)]
            v = qkv[rows, pl.ds(2 * inner + t * 128, 128)]
            heads[rows, pl.ds(t * 128, 128)] = pair_attention(q, halves(k), halves(v), mask)

    copies[3].wait()
    g2 = g2_ref[...].astype(F32)
    for t in range(width // 256):
        cols = pl.ds(t * 256, 256)
        resid_ref[:, cols] = x_ref[:, cols].astype(F32) + dot(heads[...], w2[:, cols])
    for b in range(tokens // 64):
        rows = pl.ds(b * 64, 64)
        normed[rows, :] = rms(resid_ref[rows, :], g2)

    row_flat = row_ref.shape[1]
    for i in range(3):
        copies[4 + i].wait()
        to = pl.ds(i * 256, 256)
        r = dot(normed[...], w3[:, pl.ds(i * inner, 256)]).astype(BF16)
        row_ref[:, :, to] = r.reshape(prows, row_flat, 256)
        w = dot(normed[...], w3[:, pl.ds(i * inner + 256, 256)])
        wide[0] = w[:, :128]
        wide[1] = w[:, 128:]
        for s in range(slots):
            for c in range(pcols):
                part = [
                    wide[j, pl.ds(c * slots + s, prows, stride=pcols * slots), :]
                    for j in range(2)
                ]
                col_ref[s, pl.ds(c * prows, prows), to] = jnp.concatenate(part, axis=1).astype(BF16)


def row_kernel(x_ref, o_ref, flat):
    n, each, _ = x_ref.shape
    slots = 16
    m = n * each
    block = 128
    rowi = lax.broadcasted_iota(jnp.int32, (block, m), 0)
    coli = lax.broadcasted_iota(jnp.int32, (block, m), 1)
    mask = rowi % slots == coli % slots
    x = x_ref[...].reshape(m, 3 * HR * HD)
    for t in range(HR // 2):
        k = halves(x[:, 256 + t * 128 : 384 + t * 128])
        v = halves(x[:, 512 + t * 128 : 640 + t * 128])
        for b in range(m // block):
            q = x[b * block : (b + 1) * block, t * 128 : (t + 1) * 128]
            flat[pl.ds(b * block, block), pl.ds(t * 128, 128)] = pair_attention(q, k, v, mask)
    o_ref[...] = flat[...].reshape(n, each, HR * HD)


def col_kernel(x_ref, o_ref):
    n, each, _ = x_ref.shape
    prows = 16
    pcols = each // prows
    m = n * prows
    block = 128
    for c in range(pcols):
        part = pl.ds(c * prows, prows)
        for t in range(HC // 2):
            k = halves(x_ref[:, part, pl.ds(256 + t * 128, 128)].reshape(m, 128))
            v = halves(x_ref[:, part, pl.ds(512 + t * 128, 128)].reshape(m, 128))
            for b in range(m // block):
                piece = pl.ds(b * (block // prows), block // prows)
                q = x_ref[piece, part, pl.ds(t * 128, 128)].reshape(block, 128)
                o = pair_attention(q, k, v, None)
                o_ref[piece, part, pl.ds(t * 128, 128)] = o.reshape(block // prows, prows, 128)


def mid_kernel(resid_ref, col_ref, w_ref, acc_ref, wide, natural):
    slots, each, width = col_ref.shape
    prows = 16
    pcols = each // prows
    for j in range(2):
        wide[j] = col_ref[:, :, pl.ds(j * 128, 128)].reshape(slots * each, 128).astype(F32)
    for r in range(prows):
        for c in range(pcols):
            part = [
                wide[j, pl.ds(c * prows + r, slots, stride=each), :]
                for j in range(2)
            ]
            natural[pl.ds((r * pcols + c) * slots, slots), :] = jnp.concatenate(part, axis=1).astype(BF16)
    for t in range(acc_ref.shape[1] // 256):
        cols = pl.ds(t * 256, 256)
        acc_ref[:, cols] = resid_ref[:, cols] + dot(natural[...], w_ref[:, cols])


def last_kernel(acc_ref, row_ref, w_ref, out_ref):
    m = acc_ref.shape[0]
    heads = row_ref[...].reshape(m, row_ref.shape[2])
    for t in range(acc_ref.shape[1] // 256):
        cols = pl.ds(t * 256, 256)
        out_ref[:, cols] = (acc_ref[:, cols] + dot(heads, w_ref[:, cols])).astype(BF16)


def cost(flops, nbytes, trans=0):
    return pl.CostEstimate(flops=flops, bytes_accessed=nbytes, transcendentals=trans)


def local(tokens, counts, norm_band, w_band_qkv, w_band_out, norm_space, w_space_qkv, w_space_out):
    prows, pcols, slots, width = tokens.shape
    m = prows * pcols * slots
    inner = HB * HD
    wide = 3 * HR * HD
    params = pltpu.CompilerParams(vmem_limit_bytes=48 << 20)
    resid, row_qkv, col_qkv = pl.pallas_call(
        local_kernel,
        name="local",
        out_shape=(
            jax.ShapeDtypeStruct((m, width), F32),
            jax.ShapeDtypeStruct((prows, pcols * slots, wide), BF16),
            jax.ShapeDtypeStruct((slots, pcols * prows, wide), BF16),
        ),
        in_specs=[SMEM, VMEM, VMEM, VMEM, ANY, ANY, ANY],
        out_specs=(VMEM, VMEM, VMEM),
        scratch_shapes=[
            pltpu.VMEM(w_band_qkv.shape, BF16),
            pltpu.VMEM(w_band_out.shape, BF16),
            pltpu.VMEM(w_space_qkv.shape, BF16),
            pltpu.VMEM((m, width), BF16),
            pltpu.VMEM((m, 3 * inner), BF16),
            pltpu.VMEM((m, inner), BF16),
            pltpu.VMEM((2, m, 128), F32),
            pltpu.SemaphoreType.DMA((7,)),
        ],
        compiler_params=params,
        cost_estimate=cost(2 * m * width * 4096, 12 << 20),
    )(
        counts, tokens.reshape(m, width), norm_band.reshape(1, width), norm_space.reshape(1, width),
        w_band_qkv, w_band_out, w_space_qkv,
    )
    col_all = lax.all_to_all(col_qkv, ("band", "row"), 0, 0, tiled=True)
    row_all = lax.all_to_all(row_qkv, "col", 0, 0, tiled=True)
    col_o = pl.pallas_call(
        col_kernel,
        name="column_attention",
        out_shape=jax.ShapeDtypeStruct((slots, pcols * prows, HC * HD), BF16),
        in_specs=[VMEM], out_specs=VMEM,
        compiler_params=params,
        cost_estimate=cost(1 << 28, 1 << 20),
    )(col_all)
    row_o = pl.pallas_call(
        row_kernel,
        name="row_attention",
        out_shape=jax.ShapeDtypeStruct((prows, pcols * slots, HR * HD), BF16),
        in_specs=[VMEM], out_specs=VMEM,
        scratch_shapes=[pltpu.VMEM((m, HR * HD), BF16)],
        compiler_params=params,
        cost_estimate=cost(1 << 29, 1 << 20),
    )(row_all)
    col_heads = lax.all_to_all(col_o, ("band", "row"), 0, 0, tiled=True)
    row_heads = lax.all_to_all(row_o, "col", 0, 0, tiled=True)
    acc = pl.pallas_call(
        mid_kernel,
        name="column_projection",
        out_shape=jax.ShapeDtypeStruct((m, width), F32),
        in_specs=[VMEM, VMEM, VMEM], out_specs=VMEM,
        scratch_shapes=[pltpu.VMEM((2, m, 128), F32), pltpu.VMEM((m, HC * HD), BF16)],
        compiler_params=params,
        cost_estimate=cost(2 * m * width * 256, 5 << 20),
    )(resid, col_heads, w_space_out[HR * HD :])
    out = pl.pallas_call(
        last_kernel,
        name="row_projection",
        out_shape=jax.ShapeDtypeStruct((m, width), BF16),
        in_specs=[VMEM, VMEM, VMEM], out_specs=VMEM,
        compiler_params=params,
        cost_estimate=cost(2 * m * width * 256, 5 << 20),
    )(acc, row_heads, w_space_out[: HR * HD])
    return out.reshape(prows, pcols, slots, width)


def solution(mesh):
    placed = (P(("band", "row"), "col", None, None), P(), P(), P(), P(), P(), P(), P())
    return jax.shard_map(
        local,
        mesh=mesh,
        in_specs=placed,
        out_specs=P(("band", "row"), "col", None, None),
        check_vma=False,
    )
```

```python
import jax
import jax.numpy as jnp
from jax import lax
from jax.experimental import pallas as pl
from jax.experimental.pallas import tpu as pltpu
from jax.sharding import PartitionSpec as P


HD = 64
HB = 8
HR = 4
HC = 4
EPS = 1e-06
NEG = -1e30
LOG2E = 1.4426950408889634
SCALE2 = HD**-0.5 * LOG2E
F32 = jnp.float32
BF16 = jnp.bfloat16

VMEM = pl.BlockSpec(memory_space=pltpu.VMEM)
SMEM = pl.BlockSpec(memory_space=pltpu.SMEM)
HBM = pl.BlockSpec(memory_space=pltpu.HBM)


def dot(a, b):
    return jnp.dot(a, b, preferred_element_type=F32)


def dot_t(a, b):
    return lax.dot_general(a, b, (((1,), (1,)), ((), ())), preferred_element_type=F32)


def halves(pair):
    low = lax.broadcasted_iota(jnp.int32, pair.shape, 1) < HD
    zero = jnp.zeros_like(pair)
    return jnp.concatenate([jnp.where(low, pair, zero), jnp.where(low, zero, pair)], axis=0)


def pair_attention(query, keys2, vals2, mask):
    m = query.shape[0]
    n = keys2.shape[0] // 2
    scores = dot_t(query, keys2)
    probs, totals = [], []
    for h in range(2):
        s = scores[:, h * n : (h + 1) * n]
        if mask is not None:
            s = jnp.where(mask, s, NEG)
        p = jnp.exp2((s - jnp.max(s, axis=-1, keepdims=True)) * SCALE2)
        totals.append(jnp.sum(p, axis=-1, keepdims=True))
        probs.append(p.astype(BF16))
    mixed = dot(jnp.concatenate(probs, axis=1), vals2)
    low = lax.broadcasted_iota(jnp.int32, (m, 2 * HD), 1) < HD
    return (mixed / jnp.where(low, totals[0], totals[1])).astype(BF16)


def rms(x, gain):
    scale = lax.rsqrt(jnp.mean(x * x, axis=-1, keepdims=True) + EPS)
    return (x * scale * gain).astype(BF16)


def local_kernel(
    counts_hbm, x_hbm, g1_hbm, g2_hbm, w1_hbm, w2_hbm, w3_hbm,
    resid_hbm, normed_ref, row_ref,
    counts, x_ref, g1_ref, g2_ref, w1, w2, w3, normed, qkv, heads, resid_ref, sems, wsems, rsems,
):
    prows, row_flat, _ = row_ref.shape
    tokens, width = resid_ref.shape
    slots = x_hbm.shape[2]
    inner = HB * HD
    small = [
        pltpu.make_async_copy(counts_hbm, counts, sems.at[0]),
        pltpu.make_async_copy(g1_hbm, g1_ref, sems.at[1]),
        pltpu.make_async_copy(g2_hbm, g2_ref, sems.at[2]),
    ]
    quarter = prows // 4
    loads = [
        pltpu.make_async_copy(
            x_hbm.at[pl.ds(i * quarter, quarter)], x_ref.at[pl.ds(i * quarter, quarter)], sems.at[3 + i]
        )
        for i in range(4)
    ]
    copies = []
    for i in range(3):
        cols = pl.ds(i * inner, inner)
        copies.append(pltpu.make_async_copy(w1_hbm.at[:, cols], w1.at[:, cols], wsems.at[i]))
    copies.append(pltpu.make_async_copy(w2_hbm, w2, wsems.at[3]))
    for i in range(3):
        copies.append(
            pltpu.make_async_copy(
                w3_hbm.at[:, pl.ds(i * inner, 256)], w3.at[:, pl.ds(i * 256, 256)], wsems.at[4 + i]
            )
        )
    for c in small + loads + copies:
        c.start()

    small[1].wait()
    g1 = g1_ref[...].astype(F32).reshape(1, width)
    chunk = tokens // 8
    for b in range(8):
        if b % 2 == 0:
            loads[b // 2].wait()
        rows = pl.ds(b * chunk, chunk)
        x = x_ref[pl.ds(b * prows // 8, prows // 8)].reshape(chunk, width)
        normed[rows, :] = rms(x.astype(F32), g1)
    for i in range(3):
        copies[i].wait()
        for t in range(inner // 256):
            cols = pl.ds(i * inner + t * 256, 256)
            qkv[:, cols] = dot(normed[...], w1[:, cols]).astype(BF16)

    small[0].wait()
    block = 128
    rowi = lax.broadcasted_iota(jnp.int32, (block, block), 0)
    coli = lax.broadcasted_iota(jnp.int32, (block, block), 1)
    slot = coli % slots
    ngroups = counts.shape[0]
    cap = slots // ngroups
    count = jnp.zeros((block, block), jnp.int32)
    for g in range(ngroups):
        count = jnp.where(slot // cap == g, counts[g], count)
    mask = (rowi // slots == coli // slots) & (slot % cap < count)
    for b in range(tokens // block):
        rows = pl.ds(b * block, block)
        for t in range(HB // 2):
            q = qkv[rows, pl.ds(t * 128, 128)]
            k = qkv[rows, pl.ds(inner + t * 128, 128)]
            v = qkv[rows, pl.ds(2 * inner + t * 128, 128)]
            heads[rows, pl.ds(t * 128, 128)] = pair_attention(q, halves(k), halves(v), mask)

    copies[3].wait()
    small[2].wait()
    g2 = g2_ref[...].astype(F32).reshape(1, width)
    for t in range(width // 256):
        cols = pl.ds(t * 256, 256)
        x = x_ref[:, :, :, cols].reshape(tokens, 256)
        resid_ref[:, cols] = x.astype(F32) + dot(heads[...], w2[:, cols])
    stores = [
        pltpu.make_async_copy(
            resid_ref.at[pl.ds(i * 128, 128)], resid_hbm.at[pl.ds(i * 128, 128)], rsems.at[i]
        )
        for i in range(tokens // 128)
    ]
    for c in stores:
        c.start()
    for b in range(8):
        rows = pl.ds(b * chunk, chunk)
        normed_ref[rows, :] = rms(resid_ref[rows, :], g2)

    for i in range(3):
        copies[4 + i].wait()
        to = pl.ds(i * 256, 256)
        r = dot(normed_ref[...], w3[:, to]).astype(BF16)
        row_ref[:, :, to] = r.reshape(prows, row_flat, 256)
    for c in stores:
        c.wait()


def column_qkv_kernel(me_ref, normed_ref, w3_hbm, keep_ref, send_ref, w3, wide, wsems):
    slots = 2 * keep_ref.shape[0]
    prows = slots
    pcols = keep_ref.shape[1] // prows
    inner = HB * HD
    me = me_ref[0]
    copies = [
        pltpu.make_async_copy(
            w3_hbm.at[:, pl.ds(i * inner + 256, 256)], w3.at[:, pl.ds(i * 256, 256)], wsems.at[i]
        )
        for i in range(3)
    ]
    for c in copies:
        c.start()
    for i in range(3):
        copies[i].wait()
        to = pl.ds(i * 256, 256)
        w = dot(normed_ref[...], w3[:, to])
        wide[i % 2, 0] = w[:, :128]
        wide[i % 2, 1] = w[:, 128:]
        for d in range(slots):
            ref = send_ref if d % 2 else keep_ref
            s = me ^ d
            for c in range(pcols):
                part = [
                    wide[i % 2, j, pl.ds(c * slots + s, prows, stride=pcols * slots), :]
                    for j in range(2)
                ]
                ref[d // 2, pl.ds(c * prows, prows), to] = jnp.concatenate(part, axis=1).astype(BF16)


def row_kernel(x_ref, o_ref, flat):
    n, each, _ = x_ref.shape
    slots = 16
    m = n * each
    block = 128
    rowi = lax.broadcasted_iota(jnp.int32, (block, m), 0)
    coli = lax.broadcasted_iota(jnp.int32, (block, m), 1)
    mask = rowi % slots == coli % slots
    x = x_ref[...].reshape(m, 3 * HR * HD)
    for t in range(HR // 2):
        k = halves(x[:, 256 + t * 128 : 384 + t * 128])
        v = halves(x[:, 512 + t * 128 : 640 + t * 128])
        for b in range(m // block):
            q = x[b * block : (b + 1) * block, t * 128 : (t + 1) * 128]
            flat[pl.ds(b * block, block), pl.ds(t * 128, 128)] = pair_attention(q, k, v, mask)
    o_ref[...] = flat[...].reshape(n, each, HR * HD)


def col_kernel(keep_ref, cross_ref, *refs):
    n = len(refs) // 2
    pieces, outs = refs[: n], refs[n:]
    prows = 16
    each, _ = keep_ref.shape[1:]
    pcols = each // prows
    views = [(keep_ref.at[0], cross_ref.at[0])] + [(p.at[0], p.at[1]) for p in pieces]
    flat = [v for pair in views for v in pair]
    for c in range(pcols):
        part = pl.ds(c * prows, prows)

        def take(refs_, at):
            return jnp.concatenate([r[part, pl.ds(at, 128)] for r in refs_], axis=0)

        for t in range(HC // 2):
            k = halves(take(flat, 256 + t * 128))
            v = halves(take(flat, 512 + t * 128))
            for b in range(len(flat) // 8):
                q = take(flat[b * 8 : b * 8 + 8], t * 128)
                o = pair_attention(q, k, v, None)
                for i in range(8):
                    p = b * 8 + i
                    outs[p // 2][p % 2, part, pl.ds(t * 128, 128)] = o[i * prows : (i + 1) * prows]


def mid_kernel(me_ref, resid_hbm, cross_ref, *refs):
    pieces, (w_ref, acc_ref, wide, natural, resid_ref, rsems) = refs[:8], refs[8:]
    loads = []
    for t in range(acc_ref.shape[1] // 256):
        cols = pl.ds(t * 256, 256)
        loads.append(pltpu.make_async_copy(resid_hbm.at[:, cols], resid_ref.at[:, cols], rsems.at[t]))
        loads[t].start()
    slots = 2 * len(pieces)
    each = cross_ref.shape[1]
    prows = 16
    pcols = each // prows
    me = me_ref[0]
    for d in range(slots):
        piece = cross_ref.at[d // 2] if d % 2 else pieces[d // 2].at[0]
        to = pl.ds(pl.multiple_of((me ^ d) * each, each), each)
        for j in range(2):
            wide[j, to, :] = piece[:, pl.ds(j * 128, 128)].astype(F32)
    for r in range(prows):
        for c in range(pcols):
            part = [wide[j, pl.ds(c * prows + r, slots, stride=each), :] for j in range(2)]
            natural[pl.ds((r * pcols + c) * slots, slots), :] = jnp.concatenate(part, axis=1).astype(BF16)
    for t in range(acc_ref.shape[1] // 256):
        cols = pl.ds(t * 256, 256)
        loads[t].wait()
        acc_ref[:, cols] = resid_ref[:, cols] + dot(natural[...], w_ref[:, cols])


def last_kernel(acc_ref, row_ref, w_ref, out_ref):
    m = acc_ref.shape[0]
    heads = row_ref[...].reshape(m, row_ref.shape[2])
    for t in range(acc_ref.shape[1] // 256):
        cols = pl.ds(t * 256, 256)
        out_ref[:, cols] = (acc_ref[:, cols] + dot(heads, w_ref[:, cols])).astype(BF16)


def cost(flops, nbytes, trans=0):
    return pl.CostEstimate(flops=flops, bytes_accessed=nbytes, transcendentals=trans)


def flip(array, axes, n, by):
    return lax.ppermute(array, axes, [(i, i ^ by) for i in range(n)])


def local(tokens, counts, norm_band, w_band_qkv, w_band_out, norm_space, w_space_qkv, w_space_out):
    prows, pcols, slots, width = tokens.shape
    m = prows * pcols * slots
    inner = HB * HD
    wide = 3 * HR * HD
    half = slots // 2
    each = pcols * prows
    rows_axes = ("band", "row")
    me = lax.axis_index(rows_axes).astype(jnp.int32).reshape(1)

    def params(mib):
        return pltpu.CompilerParams(vmem_limit_bytes=mib << 20)

    resid, normed, row_qkv = pl.pallas_call(
        local_kernel,
        name="local",
        out_shape=(
            jax.ShapeDtypeStruct((m, width), F32),
            jax.ShapeDtypeStruct((m, width), BF16),
            jax.ShapeDtypeStruct((prows, pcols * slots, wide), BF16),
        ),
        in_specs=[HBM] * 7,
        out_specs=(HBM, VMEM, VMEM),
        scratch_shapes=[
            pltpu.SMEM(counts.shape, jnp.int32),
            pltpu.VMEM(tokens.shape, BF16),
            pltpu.VMEM((width,), BF16),
            pltpu.VMEM((width,), BF16),
            pltpu.VMEM(w_band_qkv.shape, BF16),
            pltpu.VMEM(w_band_out.shape, BF16),
            pltpu.VMEM((width, wide), BF16),
            pltpu.VMEM((m, width), BF16),
            pltpu.VMEM((m, 3 * inner), BF16),
            pltpu.VMEM((m, inner), BF16),
            pltpu.VMEM((m, width), F32),
            pltpu.SemaphoreType.DMA((7,)),
            pltpu.SemaphoreType.DMA((7,)),
            pltpu.SemaphoreType.DMA((m // 128,)),
        ],
        compiler_params=params(59),
        cost_estimate=cost(2 * m * width * 3300, 12 << 20),
    )(counts, tokens, norm_band, norm_space, w_band_qkv, w_band_out, w_space_qkv)
    row_all = lax.all_to_all(row_qkv, "col", 0, 0, tiled=True)
    keep, send = pl.pallas_call(
        column_qkv_kernel,
        name="column_qkv",
        out_shape=(jax.ShapeDtypeStruct((half, each, wide), BF16),) * 2,
        in_specs=[SMEM, VMEM, HBM],
        out_specs=(VMEM, VMEM),
        scratch_shapes=[
            pltpu.VMEM((width, wide), BF16),
            pltpu.VMEM((2, 2, m, 128), F32),
            pltpu.SemaphoreType.DMA((3,)),
        ],
        compiler_params=params(16),
        cost_estimate=cost(2 * m * width * wide, 4 << 20),
    )(me, normed, w_space_qkv)
    cross = flip(send, rows_axes, slots, 1)
    got = []
    for d in range(1, half):
        got.append(flip(jnp.stack([keep[d], cross[d]]), rows_axes, slots, 2 * d))

    col_o = pl.pallas_call(
        col_kernel,
        name="column_attention",
        out_shape=(jax.ShapeDtypeStruct((2, each, HC * HD), BF16),) * half,
        in_specs=[VMEM] * (half + 1),
        out_specs=(VMEM,) * half,
        compiler_params=params(16),
        cost_estimate=cost(1 << 28, 1 << 20),
    )(keep, cross, *got)
    row_o = pl.pallas_call(
        row_kernel,
        name="row_attention",
        out_shape=jax.ShapeDtypeStruct((prows, pcols * slots, HR * HD), BF16),
        in_specs=[VMEM], out_specs=VMEM,
        scratch_shapes=[pltpu.VMEM((m, HR * HD), BF16)],
        compiler_params=params(16),
        cost_estimate=cost(1 << 29, 1 << 20),
    )(row_all)
    row_heads = lax.all_to_all(row_o, "col", 0, 0, tiled=True)
    back = [col_o[0]]
    for d in range(1, half):
        back.append(flip(col_o[d], rows_axes, slots, 2 * d))
    cross_back = flip(jnp.stack([b[1] for b in back]), rows_axes, slots, 1)
    acc = pl.pallas_call(
        mid_kernel,
        name="column_projection",
        out_shape=jax.ShapeDtypeStruct((m, width), F32),
        in_specs=[SMEM, HBM, VMEM] + [VMEM] * half + [VMEM], out_specs=VMEM,
        scratch_shapes=[
            pltpu.VMEM((2, m, 128), F32),
            pltpu.VMEM((m, HC * HD), BF16),
            pltpu.VMEM((m, width), F32),
            pltpu.SemaphoreType.DMA((width // 256,)),
        ],
        compiler_params=params(56),
        cost_estimate=cost(2 * m * width * 256, 5 << 20),
    )(me, resid, cross_back, *back, w_space_out[HR * HD :])
    out = pl.pallas_call(
        last_kernel,
        name="row_projection",
        out_shape=jax.ShapeDtypeStruct((m, width), BF16),
        in_specs=[VMEM, VMEM, VMEM], out_specs=VMEM,
        compiler_params=params(16),
        cost_estimate=cost(2 * m * width * 256, 5 << 20),
    )(acc, row_heads, w_space_out[: HR * HD])
    return out.reshape(prows, pcols, slots, width)


def solution(mesh):
    placed = (P(("band", "row"), "col", None, None), P(), P(), P(), P(), P(), P(), P())
    return jax.shard_map(
        local,
        mesh=mesh,
        in_specs=placed,
        out_specs=P(("band", "row"), "col", None, None),
        check_vma=False,
    )
```

```python
import jax
import jax.numpy as jnp
from jax import lax
from jax.experimental import pallas as pl
from jax.experimental.pallas import tpu as pltpu
from jax.sharding import PartitionSpec as P


HD = 64
HB = 8
HR = 4
HC = 4
EPS = 1e-06
NEG = -1e30
LOG2E = 1.4426950408889634
SCALE2 = HD**-0.5 * LOG2E
F32 = jnp.float32
BF16 = jnp.bfloat16

VMEM = pl.BlockSpec(memory_space=pltpu.VMEM)
SMEM = pl.BlockSpec(memory_space=pltpu.SMEM)
HBM = pl.BlockSpec(memory_space=pltpu.HBM)


def dot(a, b):
    return jnp.dot(a, b, preferred_element_type=F32)


def dot_t(a, b):
    return lax.dot_general(a, b, (((1,), (1,)), ((), ())), preferred_element_type=F32)


def halves(pair):
    low = lax.broadcasted_iota(jnp.int32, pair.shape, 1) < HD
    zero = jnp.zeros_like(pair)
    return jnp.concatenate([jnp.where(low, pair, zero), jnp.where(low, zero, pair)], axis=0)


def with_ones(vals2):
    n2 = vals2.shape[0]
    first = lax.broadcasted_iota(jnp.int32, (n2, 2 * HD), 0) < n2 // 2
    low = lax.broadcasted_iota(jnp.int32, (n2, 2 * HD), 1) < HD
    ones = jnp.where(first == low, 1.0, 0.0).astype(BF16)
    return jnp.concatenate([vals2, ones], axis=1)


def pair_attention(query, keys2, vals2, mask):
    n = keys2.shape[0] // 2
    scores = dot_t(query, keys2)
    probs = []
    for h in range(2):
        s = scores[:, h * n : (h + 1) * n]
        if mask is not None:
            s = jnp.where(mask, s, NEG)
        p = jnp.exp2((s - jnp.max(s, axis=-1, keepdims=True)) * SCALE2)
        probs.append(p.astype(BF16))
    mixed = dot(jnp.concatenate(probs, axis=1), vals2)
    return (mixed[:, : 2 * HD] / mixed[:, 2 * HD :]).astype(BF16)


def rms(x, gain):
    scale = lax.rsqrt(jnp.mean(x * x, axis=-1, keepdims=True) + EPS)
    return (x * scale * gain).astype(BF16)


def local_kernel(
    counts_hbm, x_hbm, g1_hbm, g2_hbm, w1_hbm, w2_hbm, w3_hbm, me_ref,
    resid_hbm, row_hbm, *refs,
):
    chips = 8
    cols_hbm = refs[:chips]
    (
        counts, x_ref, g1_ref, g2_ref, w1, w2, w3, normed, qkv, heads,
        resid_ref, row_ref, col_ref, wide, sems, wsems, osems,
    ) = refs[chips:]
    prows, row_flat, _ = row_ref.shape
    tokens, width = resid_ref.shape
    slots = x_hbm.shape[2]
    pcols = x_hbm.shape[1]
    inner = HB * HD
    chip = me_ref[0] // 2
    small = [
        pltpu.make_async_copy(g1_hbm, g1_ref, sems.at[1]),
        pltpu.make_async_copy(g2_hbm, g2_ref, sems.at[2]),
        pltpu.make_async_copy(counts_hbm, counts, sems.at[0]),
    ]
    quarter = prows // 4
    loads = [
        pltpu.make_async_copy(
            x_hbm.at[pl.ds(i * quarter, quarter)], x_ref.at[pl.ds(i * quarter, quarter)], sems.at[3 + i]
        )
        for i in range(4)
    ]
    copies = []
    for i in range(3):
        cols = pl.ds(i * inner, inner)
        copies.append(pltpu.make_async_copy(w1_hbm.at[:, cols], w1.at[:, cols], wsems.at[i]))
    copies.append(pltpu.make_async_copy(w2_hbm, w2, wsems.at[3]))
    for i in range(3):
        cols = pl.ds(i * inner, inner)
        copies.append(pltpu.make_async_copy(w3_hbm.at[:, cols], w3.at[:, cols], wsems.at[4 + i]))
    small[0].start()
    for c in loads + copies[:1] + small[1:] + copies[1:3]:
        c.start()

    small[0].wait()
    g1 = g1_ref[...].astype(F32).reshape(1, width)
    for b in range(tokens // 16):
        if b % (2 * quarter) == 0:
            loads[b // (2 * quarter)].wait()
        normed[pl.ds(b * 16, 16), :] = rms(x_ref[b // pcols, b % pcols].astype(F32), g1)
    for c in copies[3:]:
        c.start()
    for i in range(3):
        copies[i].wait()
        for t in range(inner // 256):
            cols = pl.ds(i * inner + t * 256, 256)
            qkv[:, cols] = dot(normed[...], w1[:, cols]).astype(BF16)

    small[2].wait()
    block = 128
    rowi = lax.broadcasted_iota(jnp.int32, (block, block), 0)
    coli = lax.broadcasted_iota(jnp.int32, (block, block), 1)
    slot = coli % slots
    ngroups = counts.shape[0]
    cap = slots // ngroups
    count = jnp.zeros((block, block), jnp.int32)
    for g in range(ngroups):
        count = jnp.where(slot // cap == g, counts[g], count)
    mask = (rowi // slots == coli // slots) & (slot % cap < count)
    for b in range(tokens // block):
        rows = pl.ds(b * block, block)
        for t in range(HB // 2):
            q = qkv[rows, pl.ds(t * 128, 128)]
            k = qkv[rows, pl.ds(inner + t * 128, 128)]
            v = qkv[rows, pl.ds(2 * inner + t * 128, 128)]
            heads[rows, pl.ds(t * 128, 128)] = pair_attention(q, halves(k), with_ones(halves(v)), mask)

    for c in copies[3:]:
        c.wait()
    small[1].wait()
    g2 = g2_ref[...].astype(F32).reshape(1, width)
    for t in range(width // 256):
        cols = pl.ds(t * 256, 256)
        x = x_ref[:, :, :, cols].reshape(tokens, 256)
        resid_ref[:, cols] = x.astype(F32) + dot(heads[...], w2[:, cols])
    stores = [pltpu.make_async_copy(resid_ref, resid_hbm, osems.at[0])]
    stores[0].start()
    for b in range(tokens // 16):
        rows = pl.ds(b * 16, 16)
        normed[rows, :] = rms(resid_ref[rows, :], g2)

    for i in range(3):
        to = pl.ds(i * 256, 256)
        w = dot(normed[...], w3[:, pl.ds(i * inner + 256, 256)])
        wide[i % 2, 0] = w[:, :128]
        wide[i % 2, 1] = w[:, 128:]
        for d in range(chips):
            for low in range(2):
                s = 2 * (chip ^ d) + low
                for c in range(pcols):
                    part = [
                        wide[i % 2, j, pl.ds(c * slots + s, prows, stride=pcols * slots), :]
                        for j in range(2)
                    ]
                    at = pl.ds((low * pcols + c) * prows, prows)
                    col_ref[d, at, to] = jnp.concatenate(part, axis=1).astype(BF16)
    for d in range(chips):
        stores.append(pltpu.make_async_copy(col_ref.at[d], cols_hbm[d], osems.at[1 + d]))
        stores[-1].start()
    for i in range(3):
        to = pl.ds(i * 256, 256)
        r = dot(normed[...], w3[:, pl.ds(i * inner, 256)]).astype(BF16)
        row_ref[:, :, to] = r.reshape(prows, row_flat, 256)
        stores.append(
            pltpu.make_async_copy(row_ref.at[:, :, to], row_hbm.at[:, :, to], osems.at[1 + chips + i])
        )
        stores[-1].start()
    for c in stores:
        c.wait()


def row_kernel(x_ref, o_ref, flat):
    n, each, _ = x_ref.shape
    slots = 16
    m = n * each
    block = 128
    rowi = lax.broadcasted_iota(jnp.int32, (block, m), 0)
    coli = lax.broadcasted_iota(jnp.int32, (block, m), 1)
    mask = rowi % slots == coli % slots
    x = x_ref[...].reshape(m, 3 * HR * HD)
    for t in range(HR // 2):
        k = halves(x[:, 256 + t * 128 : 384 + t * 128])
        v = with_ones(halves(x[:, 512 + t * 128 : 640 + t * 128]))
        for b in range(m // block):
            q = x[b * block : (b + 1) * block, t * 128 : (t + 1) * 128]
            flat[pl.ds(b * block, block), pl.ds(t * 128, 128)] = pair_attention(q, k, v, mask)
    o_ref[...] = flat[...].reshape(n, each, HR * HD)


def col_kernel(own_ref, cross_ref, *refs):
    n = len(refs) // 2
    pieces, outs = (own_ref,) + refs[:n], refs[n:]
    prows = 16
    each = cross_ref.shape[1]
    others = [cross_ref.at[d] for d in range(len(pieces))]
    for g in range(each // prows):
        part = pl.ds(g * prows, prows)

        def take(refs_, at):
            return jnp.concatenate([r[part, pl.ds(at, 128)] for r in refs_], axis=0)

        for t in range(HC // 2):
            at = t * 128
            k = halves(jnp.concatenate([take(pieces, 256 + at), take(others, at)], axis=0))
            v = with_ones(halves(jnp.concatenate([take(pieces, 512 + at), take(others, 256 + at)], axis=0)))
            o = pair_attention(take(pieces, at), k, v, None)
            for d in range(len(pieces)):
                outs[d][part, pl.ds(at, 128)] = o[d * prows : (d + 1) * prows]


def mid_kernel(me_ref, resid_hbm, *refs):
    pieces, (w_ref, acc_ref, wide, natural, resid_ref, rsems) = refs[:8], refs[8:]
    loads = []
    for t in range(acc_ref.shape[1] // 256):
        cols = pl.ds(t * 256, 256)
        loads.append(pltpu.make_async_copy(resid_hbm.at[:, cols], resid_ref.at[:, cols], rsems.at[t]))
        loads[t].start()
    slots = 2 * len(pieces)
    each = pieces[0].shape[0]
    prows = 16
    pcols = each // 2 // prows
    chip = me_ref[0] // 2
    for d in range(len(pieces)):
        to = pl.ds(pl.multiple_of((chip ^ d) * each, each), each)
        for j in range(2):
            wide[j, to, :] = pieces[d][:, pl.ds(j * 128, 128)].astype(F32)
    for r in range(prows):
        for c in range(pcols):
            part = [
                wide[j, pl.ds(c * prows + r, slots, stride=pcols * prows), :] for j in range(2)
            ]
            natural[pl.ds((r * pcols + c) * slots, slots), :] = jnp.concatenate(part, axis=1).astype(BF16)
    for t in range(acc_ref.shape[1] // 256):
        cols = pl.ds(t * 256, 256)
        loads[t].wait()
        acc_ref[:, cols] = resid_ref[:, cols] + dot(natural[...], w_ref[:, cols])


def last_kernel(acc_ref, row_ref, w_ref, out_ref):
    m = acc_ref.shape[0]
    heads = row_ref[...].reshape(m, row_ref.shape[2])
    for t in range(acc_ref.shape[1] // 256):
        cols = pl.ds(t * 256, 256)
        out_ref[:, cols] = (acc_ref[:, cols] + dot(heads, w_ref[:, cols])).astype(BF16)


def cost(flops, nbytes, trans=0):
    return pl.CostEstimate(flops=flops, bytes_accessed=nbytes, transcendentals=trans)


def flip(array, axes, n, by):
    return lax.ppermute(array, axes, [(i, i ^ by) for i in range(n)])


def local(tokens, counts, norm_band, w_band_qkv, w_band_out, norm_space, w_space_qkv, w_space_out):
    prows, pcols, slots, width = tokens.shape
    m = prows * pcols * slots
    inner = HB * HD
    wide = 3 * HR * HD
    half = slots // 2
    each = 2 * pcols * prows
    rows_axes = ("band", "row")
    me = lax.axis_index(rows_axes).astype(jnp.int32).reshape(1)

    def params(mib):
        return pltpu.CompilerParams(vmem_limit_bytes=mib << 20)

    resid, row_qkv, *col_qkv = pl.pallas_call(
        local_kernel,
        name="local",
        out_shape=(jax.ShapeDtypeStruct((m, width), F32), jax.ShapeDtypeStruct((prows, pcols * slots, wide), BF16))
        + (jax.ShapeDtypeStruct((each, wide), BF16),) * half,
        in_specs=[HBM] * 7 + [SMEM],
        out_specs=(HBM,) * (2 + half),
        scratch_shapes=[
            pltpu.SMEM(counts.shape, jnp.int32),
            pltpu.VMEM(tokens.shape, BF16),
            pltpu.VMEM((width,), BF16),
            pltpu.VMEM((width,), BF16),
            pltpu.VMEM(w_band_qkv.shape, BF16),
            pltpu.VMEM(w_band_out.shape, BF16),
            pltpu.VMEM(w_space_qkv.shape, BF16),
            pltpu.VMEM((m, width), BF16),
            pltpu.VMEM((m, 3 * inner), BF16),
            pltpu.VMEM((m, inner), BF16),
            pltpu.VMEM((m, width), F32),
            pltpu.VMEM((prows, pcols * slots, wide), BF16),
            pltpu.VMEM((half, each, wide), BF16),
            pltpu.VMEM((2, 2, m, 128), F32),
            pltpu.SemaphoreType.DMA((7,)),
            pltpu.SemaphoreType.DMA((7,)),
            pltpu.SemaphoreType.DMA((4 + half,)),
        ],
        compiler_params=params(59),
        cost_estimate=cost(2 * m * width * 4096, 12 << 20),
    )(counts, tokens, norm_band, norm_space, w_band_qkv, w_band_out, w_space_qkv, me)
    row_all = lax.all_to_all(row_qkv, "col", 0, 0, tiled=True)
    got = []
    for d in range(1, half):
        got.append(flip(col_qkv[d], rows_axes, slots, 2 * d))
    pack = jnp.stack([g[:, HC * HD :] for g in [col_qkv[0]] + got])
    cross = flip(pack, rows_axes, slots, 1)
    row_o = pl.pallas_call(
        row_kernel,
        name="row_attention",
        out_shape=jax.ShapeDtypeStruct((prows, pcols * slots, HR * HD), BF16),
        in_specs=[VMEM], out_specs=VMEM,
        scratch_shapes=[pltpu.VMEM((m, HR * HD), BF16)],
        compiler_params=params(16),
        cost_estimate=cost(1 << 29, 1 << 20),
    )(row_all)
    row_heads = lax.all_to_all(row_o, "col", 0, 0, tiled=True)
    col_o = pl.pallas_call(
        col_kernel,
        name="column_attention",
        out_shape=(jax.ShapeDtypeStruct((each, HC * HD), BF16),) * half,
        in_specs=[VMEM] * (half + 1),
        out_specs=(VMEM,) * half,
        compiler_params=params(16),
        cost_estimate=cost(1 << 28, 1 << 20),
    )(col_qkv[0], cross, *got)
    back = [col_o[0]]
    for d in range(1, half):
        back.append(flip(col_o[d], rows_axes, slots, 2 * d))
    acc = pl.pallas_call(
        mid_kernel,
        name="column_projection",
        out_shape=jax.ShapeDtypeStruct((m, width), F32),
        in_specs=[SMEM, HBM] + [VMEM] * half + [VMEM], out_specs=VMEM,
        scratch_shapes=[
            pltpu.VMEM((2, m, 128), F32),
            pltpu.VMEM((m, HC * HD), BF16),
            pltpu.VMEM((m, width), F32),
            pltpu.SemaphoreType.DMA((width // 256,)),
        ],
        compiler_params=params(16),
        cost_estimate=cost(2 * m * width * 256, 5 << 20),
    )(me, resid, *back, w_space_out[HR * HD :])
    out = pl.pallas_call(
        last_kernel,
        name="row_projection",
        out_shape=jax.ShapeDtypeStruct((m, width), BF16),
        in_specs=[VMEM, VMEM, VMEM], out_specs=VMEM,
        compiler_params=params(16),
        cost_estimate=cost(2 * m * width * 256, 5 << 20),
    )(acc, row_heads, w_space_out[: HR * HD])
    return out.reshape(prows, pcols, slots, width)


def solution(mesh):
    placed = (P(("band", "row"), "col", None, None), P(), P(), P(), P(), P(), P(), P())
    return jax.shard_map(
        local,
        mesh=mesh,
        in_specs=placed,
        out_specs=P(("band", "row"), "col", None, None),
        check_vma=False,
    )
```

```python
import jax
import jax.numpy as jnp
from jax import lax
from jax.experimental import pallas as pl
from jax.experimental.pallas import tpu as pltpu
from jax.sharding import PartitionSpec as P


HD = 64
HB = 8
HR = 4
HC = 4
EPS = 1e-06
NEG = -1e30
LOG2E = 1.4426950408889634
SCALE2 = HD**-0.5 * LOG2E
F32 = jnp.float32
BF16 = jnp.bfloat16

VMEM = pl.BlockSpec(memory_space=pltpu.VMEM)
SMEM = pl.BlockSpec(memory_space=pltpu.SMEM)
HBM = pl.BlockSpec(memory_space=pltpu.HBM)


def dot(a, b):
    return jnp.dot(a, b, preferred_element_type=F32)


def dot_t(a, b):
    return lax.dot_general(a, b, (((1,), (1,)), ((), ())), preferred_element_type=F32)


def halves(pair):
    low = lax.broadcasted_iota(jnp.int32, pair.shape, 1) < HD
    zero = jnp.zeros_like(pair)
    return jnp.concatenate([jnp.where(low, pair, zero), jnp.where(low, zero, pair)], axis=0)


def with_ones(vals2):
    n2 = vals2.shape[0]
    first = lax.broadcasted_iota(jnp.int32, (n2, 2 * HD), 0) < n2 // 2
    low = lax.broadcasted_iota(jnp.int32, (n2, 2 * HD), 1) < HD
    ones = jnp.where(first == low, 1.0, 0.0).astype(BF16)
    return jnp.concatenate([vals2, ones], axis=1)


def pair_attention(query, keys2, vals2, mask):
    n = keys2.shape[0] // 2
    scores = dot_t(query, keys2)
    probs = []
    for h in range(2):
        s = scores[:, h * n : (h + 1) * n]
        if mask is not None:
            s = jnp.where(mask, s, NEG)
        p = jnp.exp2((s - jnp.max(s, axis=-1, keepdims=True)) * SCALE2)
        probs.append(p.astype(BF16))
    mixed = dot(jnp.concatenate(probs, axis=1), vals2)
    return (mixed[:, : 2 * HD] / mixed[:, 2 * HD :]).astype(BF16)


def rms(x, gain):
    scale = lax.rsqrt(jnp.mean(x * x, axis=-1, keepdims=True) + EPS)
    return (x * scale * gain).astype(BF16)


def local_kernel(
    counts_hbm, x_hbm, g1_hbm, g2_hbm, w1_hbm, w2_hbm, w3_hbm, me_ref,
    resid_hbm, row_hbm, *refs,
):
    chips = 4
    cols_hbm, kv_hbm = refs[:chips], refs[chips]
    (
        counts, x_ref, g1_ref, g2_ref, w1, w2, w3, normed, qkv, heads,
        resid_ref, row_ref, col_ref, wide, sems, wsems, osems,
    ) = refs[chips + 1 :]
    prows, row_flat, _ = row_ref.shape
    tokens, width = resid_ref.shape
    slots = x_hbm.shape[2]
    pcols = x_hbm.shape[1]
    inner = HB * HD
    each_slots = slots // chips
    chip = me_ref[0] // 4
    small = [
        pltpu.make_async_copy(g1_hbm, g1_ref, sems.at[1]),
        pltpu.make_async_copy(g2_hbm, g2_ref, sems.at[2]),
        pltpu.make_async_copy(counts_hbm, counts, sems.at[0]),
    ]
    quarter = prows // 4
    loads = [
        pltpu.make_async_copy(
            x_hbm.at[pl.ds(i * quarter, quarter)], x_ref.at[pl.ds(i * quarter, quarter)], sems.at[3 + i]
        )
        for i in range(4)
    ]
    copies = []
    for i in range(3):
        cols = pl.ds(i * inner, inner)
        copies.append(pltpu.make_async_copy(w1_hbm.at[:, cols], w1.at[:, cols], wsems.at[i]))
    copies.append(pltpu.make_async_copy(w2_hbm, w2, wsems.at[3]))
    for i in range(3):
        cols = pl.ds(i * inner, inner)
        copies.append(pltpu.make_async_copy(w3_hbm.at[:, cols], w3.at[:, cols], wsems.at[4 + i]))
    small[0].start()
    for c in loads + copies[:1] + small[1:] + copies[1:3]:
        c.start()

    small[0].wait()
    g1 = g1_ref[...].astype(F32).reshape(1, width)
    for b in range(tokens // 16):
        if b % (2 * quarter) == 0:
            loads[b // (2 * quarter)].wait()
        normed[pl.ds(b * 16, 16), :] = rms(x_ref[b // pcols, b % pcols].astype(F32), g1)
    for c in copies[3:]:
        c.start()
    for i in range(3):
        copies[i].wait()
        for t in range(inner // 256):
            cols = pl.ds(i * inner + t * 256, 256)
            qkv[:, cols] = dot(normed[...], w1[:, cols]).astype(BF16)

    small[2].wait()
    block = 128
    rowi = lax.broadcasted_iota(jnp.int32, (block, block), 0)
    coli = lax.broadcasted_iota(jnp.int32, (block, block), 1)
    slot = coli % slots
    ngroups = counts.shape[0]
    cap = slots // ngroups
    count = jnp.zeros((block, block), jnp.int32)
    for g in range(ngroups):
        count = jnp.where(slot // cap == g, counts[g], count)
    mask = (rowi // slots == coli // slots) & (slot % cap < count)
    for b in range(tokens // block):
        rows = pl.ds(b * block, block)
        for t in range(HB // 2):
            q = qkv[rows, pl.ds(t * 128, 128)]
            k = qkv[rows, pl.ds(inner + t * 128, 128)]
            v = qkv[rows, pl.ds(2 * inner + t * 128, 128)]
            heads[rows, pl.ds(t * 128, 128)] = pair_attention(q, halves(k), with_ones(halves(v)), mask)

    for c in copies[3:]:
        c.wait()
    small[1].wait()
    g2 = g2_ref[...].astype(F32).reshape(1, width)
    for t in range(width // 256):
        cols = pl.ds(t * 256, 256)
        x = x_ref[:, :, :, cols].reshape(tokens, 256)
        resid_ref[:, cols] = x.astype(F32) + dot(heads[...], w2[:, cols])
    stores = [pltpu.make_async_copy(resid_ref, resid_hbm, osems.at[0])]
    stores[0].start()
    for b in range(tokens // 16):
        rows = pl.ds(b * 16, 16)
        normed[rows, :] = rms(resid_ref[rows, :], g2)

    for i in range(3):
        to = pl.ds(i * 256, 256)
        w = dot(normed[...], w3[:, pl.ds(i * inner + 256, 256)])
        wide[i % 2, 0] = w[:, :128]
        wide[i % 2, 1] = w[:, 128:]
        for d in range(chips):
            for low in range(each_slots):
                s = each_slots * (chip ^ d) + low
                for c in range(pcols):
                    part = [
                        wide[i % 2, j, pl.ds(c * slots + s, prows, stride=pcols * slots), :]
                        for j in range(2)
                    ]
                    at = pl.ds((low * pcols + c) * prows, prows)
                    col_ref[d, at, to] = jnp.concatenate(part, axis=1).astype(BF16)
    for d in range(chips):
        stores.append(pltpu.make_async_copy(col_ref.at[d], cols_hbm[d], osems.at[1 + d]))
        stores[-1].start()
    kv = pl.ds(HC * HD, 2 * HC * HD)
    stores.append(pltpu.make_async_copy(col_ref.at[0, :, kv], kv_hbm, osems.at[1 + chips]))
    stores[-1].start()
    for i in range(3):
        to = pl.ds(i * 256, 256)
        r = dot(normed[...], w3[:, pl.ds(i * inner, 256)]).astype(BF16)
        row_ref[:, :, to] = r.reshape(prows, row_flat, 256)
        stores.append(
            pltpu.make_async_copy(row_ref.at[:, :, to], row_hbm.at[:, :, to], osems.at[2 + chips + i])
        )
        stores[-1].start()
    for c in stores:
        c.wait()


def row_kernel(x_ref, o_ref, flat):
    n, each, _ = x_ref.shape
    slots = 16
    m = n * each
    block = 128
    rowi = lax.broadcasted_iota(jnp.int32, (block, m), 0)
    coli = lax.broadcasted_iota(jnp.int32, (block, m), 1)
    mask = rowi % slots == coli % slots
    x = x_ref[...].reshape(m, 3 * HR * HD)
    for t in range(HR // 2):
        k = halves(x[:, 256 + t * 128 : 384 + t * 128])
        v = with_ones(halves(x[:, 512 + t * 128 : 640 + t * 128]))
        for b in range(m // block):
            q = x[b * block : (b + 1) * block, t * 128 : (t + 1) * 128]
            flat[pl.ds(b * block, block), pl.ds(t * 128, 128)] = pair_attention(q, k, v, mask)
    o_ref[...] = flat[...].reshape(n, each, HR * HD)


def col_kernel(*refs):
    n = 4
    pieces, others, outs = refs[:n], refs[n : 4 * n], refs[4 * n :]
    prows = 16
    each = pieces[0].shape[0]
    for g in range(each // prows):
        part = pl.ds(g * prows, prows)

        def take(refs_, at):
            return [r[part, pl.ds(at, 128)] for r in refs_]

        for t in range(HC // 2):
            at = t * 128
            k = jnp.concatenate(take(pieces, 256 + at) + take(others, at), axis=0)
            v = jnp.concatenate(take(pieces, 512 + at) + take(others, 256 + at), axis=0)
            q = jnp.concatenate(take(pieces, at), axis=0)
            o = pair_attention(q, halves(k), with_ones(halves(v)), None)
            for d in range(n):
                outs[d][part, pl.ds(at, 128)] = o[d * prows : (d + 1) * prows]


def mid_kernel(me_ref, resid_hbm, p0, p1, p2, p3, w_ref, acc_ref, wide, natural, resid_ref, rsems):
    pieces = (p0, p1, p2, p3)
    loads = []
    for t in range(acc_ref.shape[1] // 256):
        cols = pl.ds(t * 256, 256)
        loads.append(pltpu.make_async_copy(resid_hbm.at[:, cols], resid_ref.at[:, cols], rsems.at[t]))
        loads[t].start()
    slots = prows = 16
    each = pieces[0].shape[0]
    pcols = each * len(pieces) // slots // prows
    chip = me_ref[0] // 4
    for d in range(len(pieces)):
        to = pl.ds(pl.multiple_of((chip ^ d) * each, each), each)
        for j in range(2):
            wide[j, to, :] = pieces[d][:, pl.ds(j * 128, 128)].astype(F32)
    for r in range(prows):
        for c in range(pcols):
            part = [
                wide[j, pl.ds(c * prows + r, slots, stride=pcols * prows), :] for j in range(2)
            ]
            natural[pl.ds((r * pcols + c) * slots, slots), :] = jnp.concatenate(part, axis=1).astype(BF16)
    for t in range(acc_ref.shape[1] // 256):
        cols = pl.ds(t * 256, 256)
        loads[t].wait()
        acc_ref[:, cols] = resid_ref[:, cols] + dot(natural[...], w_ref[:, cols])


def last_kernel(acc_ref, row_ref, w_ref, out_hbm, out_ref, sems):
    m = acc_ref.shape[0]
    n = sems.shape[0]
    stores = []
    for i in range(n):
        rows = pl.ds(i * (m // n), m // n)
        heads = row_ref[pl.ds(i * (row_ref.shape[0] // n), row_ref.shape[0] // n)]
        heads = heads.reshape(m // n, row_ref.shape[2])
        out_ref[rows, :] = (acc_ref[rows, :] + dot(heads, w_ref[...])).astype(BF16)
        stores.append(pltpu.make_async_copy(out_ref.at[rows], out_hbm.at[rows], sems.at[i]))
        stores[i].start()
    for c in stores:
        c.wait()


def cost(flops, nbytes, trans=0):
    return pl.CostEstimate(flops=flops, bytes_accessed=nbytes, transcendentals=trans)


def flip(array, axes, n, by):
    return lax.ppermute(array, axes, [(i, i ^ by) for i in range(n)])


def local(tokens, counts, norm_band, w_band_qkv, w_band_out, norm_space, w_space_qkv, w_space_out):
    prows, pcols, slots, width = tokens.shape
    m = prows * pcols * slots
    inner = HB * HD
    wide = 3 * HR * HD
    xn = 4
    each = slots // xn * pcols * prows
    kv_wide = 2 * HC * HD
    rows_axes = ("band", "row")
    me = lax.axis_index(rows_axes).astype(jnp.int32).reshape(1)

    def params(mib):
        return pltpu.CompilerParams(vmem_limit_bytes=mib << 20)

    resid, row_qkv, *col_qkv, kv0 = pl.pallas_call(
        local_kernel,
        name="local",
        out_shape=(jax.ShapeDtypeStruct((m, width), F32), jax.ShapeDtypeStruct((prows, pcols * slots, wide), BF16))
        + (jax.ShapeDtypeStruct((each, wide), BF16),) * xn
        + (jax.ShapeDtypeStruct((each, kv_wide), BF16),),
        in_specs=[HBM] * 7 + [SMEM],
        out_specs=(HBM,) * (3 + xn),
        scratch_shapes=[
            pltpu.SMEM(counts.shape, jnp.int32),
            pltpu.VMEM(tokens.shape, BF16),
            pltpu.VMEM((width,), BF16),
            pltpu.VMEM((width,), BF16),
            pltpu.VMEM(w_band_qkv.shape, BF16),
            pltpu.VMEM(w_band_out.shape, BF16),
            pltpu.VMEM(w_space_qkv.shape, BF16),
            pltpu.VMEM((m, width), BF16),
            pltpu.VMEM((m, 3 * inner), BF16),
            pltpu.VMEM((m, inner), BF16),
            pltpu.VMEM((m, width), F32),
            pltpu.VMEM((prows, pcols * slots, wide), BF16),
            pltpu.VMEM((xn, each, wide), BF16),
            pltpu.VMEM((2, 2, m, 128), F32),
            pltpu.SemaphoreType.DMA((7,)),
            pltpu.SemaphoreType.DMA((7,)),
            pltpu.SemaphoreType.DMA((5 + xn,)),
        ],
        compiler_params=params(59),
        cost_estimate=cost(2 * m * width * 4096, 12 << 20),
    )(counts, tokens, norm_band, norm_space, w_band_qkv, w_band_out, w_space_qkv, me)
    row_all = lax.all_to_all(row_qkv, "col", 0, 0, tiled=True)
    pieces, kvs = [col_qkv[0]], [kv0]
    for d in range(1, xn):
        pieces.append(flip(col_qkv[d], rows_axes, slots, 4 * d))
        kvs.append(pieces[d][:, HC * HD :])
    far, core, core_far = [], [], []
    for d in range(xn):
        far.append(flip(kvs[d], rows_axes, slots, 2))
        core.append(flip(kvs[d], rows_axes, slots, 1))
        core_far.append(flip(far[d], rows_axes, slots, 1))
    row_o = pl.pallas_call(
        row_kernel,
        name="row_attention",
        out_shape=jax.ShapeDtypeStruct((prows, pcols * slots, HR * HD), BF16),
        in_specs=[VMEM], out_specs=VMEM,
        scratch_shapes=[pltpu.VMEM((m, HR * HD), BF16)],
        compiler_params=params(16),
        cost_estimate=cost(1 << 29, 1 << 20),
    )(row_all)
    row_heads = lax.all_to_all(row_o, "col", 0, 0, tiled=True)
    col_o = pl.pallas_call(
        col_kernel,
        name="column_attention",
        out_shape=(jax.ShapeDtypeStruct((each, HC * HD), BF16),) * xn,
        in_specs=[VMEM] * (4 * xn),
        out_specs=(VMEM,) * xn,
        compiler_params=params(16),
        cost_estimate=cost(1 << 28, 1 << 20),
    )(*pieces, *far, *core, *core_far)
    back = [col_o[0]]
    for d in range(1, xn):
        back.append(flip(col_o[d], rows_axes, slots, 4 * d))
    acc = pl.pallas_call(
        mid_kernel,
        name="column_projection",
        out_shape=jax.ShapeDtypeStruct((m, width), F32),
        in_specs=[SMEM, HBM] + [VMEM] * (xn + 1), out_specs=VMEM,
        scratch_shapes=[
            pltpu.VMEM((2, m, 128), F32),
            pltpu.VMEM((m, HC * HD), BF16),
            pltpu.VMEM((m, width), F32),
            pltpu.SemaphoreType.DMA((width // 256,)),
        ],
        compiler_params=params(50),
        cost_estimate=cost(2 * m * width * 256, 5 << 20),
    )(me, resid, *back, w_space_out[HR * HD :])
    out = pl.pallas_call(
        last_kernel,
        name="row_projection",
        out_shape=jax.ShapeDtypeStruct((m, width), BF16),
        in_specs=[VMEM, VMEM, VMEM], out_specs=HBM,
        scratch_shapes=[pltpu.VMEM((m, width), BF16), pltpu.SemaphoreType.DMA((4,))],
        compiler_params=params(16),
        cost_estimate=cost(2 * m * width * 256, 5 << 20),
    )(acc, row_heads, w_space_out[: HR * HD])
    return out.reshape(prows, pcols, slots, width)


def solution(mesh):
    placed = (P(("band", "row"), "col", None, None), P(), P(), P(), P(), P(), P(), P())
    return jax.shard_map(
        local,
        mesh=mesh,
        in_specs=placed,
        out_specs=P(("band", "row"), "col", None, None),
        check_vma=False,
    )
```

```python
import jax
import jax.numpy as jnp
from jax import lax
from jax.experimental import pallas as pl
from jax.experimental.pallas import tpu as pltpu
from jax.sharding import PartitionSpec as P


HD = 64
HB = 8
HR = 4
HC = 4
EPS = 1e-06
NEG = -1e30
LOG2E = 1.4426950408889634
SCALE2 = HD**-0.5 * LOG2E
F32 = jnp.float32
BF16 = jnp.bfloat16

VMEM = pl.BlockSpec(memory_space=pltpu.VMEM)
SMEM = pl.BlockSpec(memory_space=pltpu.SMEM)
HBM = pl.BlockSpec(memory_space=pltpu.HBM)


def dot(a, b):
    return jnp.dot(a, b, preferred_element_type=F32)


def dot_t(a, b):
    return lax.dot_general(a, b, (((1,), (1,)), ((), ())), preferred_element_type=F32)


def halves(pair):
    low = lax.broadcasted_iota(jnp.int32, pair.shape, 1) < HD
    zero = jnp.zeros_like(pair)
    return jnp.concatenate([jnp.where(low, pair, zero), jnp.where(low, zero, pair)], axis=0)


def with_ones(vals2):
    n2 = vals2.shape[0]
    first = lax.broadcasted_iota(jnp.int32, (n2, 2 * HD), 0) < n2 // 2
    low = lax.broadcasted_iota(jnp.int32, (n2, 2 * HD), 1) < HD
    ones = jnp.where(first == low, 1.0, 0.0).astype(BF16)
    return jnp.concatenate([vals2, ones], axis=1)


def pair_attention(query, keys2, vals2, mask):
    n = keys2.shape[0] // 2
    scores = dot_t(query, keys2)
    probs = []
    for h in range(2):
        s = scores[:, h * n : (h + 1) * n]
        if mask is not None:
            s = jnp.where(mask, s, NEG)
        p = jnp.exp2((s - jnp.max(s, axis=-1, keepdims=True)) * SCALE2)
        probs.append(p.astype(BF16))
    mixed = dot(jnp.concatenate(probs, axis=1), vals2)
    return (mixed[:, : 2 * HD] / mixed[:, 2 * HD :]).astype(BF16)


def stacked_attention(query, keys, vals, mask):
    m = query.shape[0]
    scores = dot_t(halves(query), keys)
    probs = []
    for h in range(2):
        s = scores[h * m : (h + 1) * m]
        if mask is not None:
            s = jnp.where(mask, s, NEG)
        p = jnp.exp2((s - jnp.max(s, axis=-1, keepdims=True)) * SCALE2)
        probs.append(p.astype(BF16))
    both = jnp.concatenate([vals, jnp.ones_like(vals)], axis=1)
    mixed = dot(jnp.concatenate(probs, axis=0), both)
    low = lax.broadcasted_iota(jnp.int32, (m, 2 * HD), 1) < HD
    heads = jnp.where(low, mixed[:m, : 2 * HD], mixed[m:, : 2 * HD])
    return (heads / jnp.where(low, mixed[:m, 2 * HD :], mixed[m:, 2 * HD :])).astype(BF16)


def rms(x, gain):
    scale = lax.rsqrt(jnp.mean(x * x, axis=-1, keepdims=True) + EPS)
    return (x * scale * gain).astype(BF16)


def local_kernel(
    counts_hbm, x_hbm, g1_hbm, g2_hbm, w1_hbm, w2_hbm, w3_hbm, me_ref,
    resid_hbm, row_hbm, *refs,
):
    chips = 4
    cols_hbm, kv_hbm = refs[:chips], refs[chips]
    (
        counts, x_ref, g1_ref, g2_ref, w1, w2, w3, normed, qkv, heads,
        resid_ref, row_ref, col_ref, wide, sems, wsems, osems,
    ) = refs[chips + 1 :]
    prows, row_flat, _ = row_ref.shape
    tokens, width = resid_ref.shape
    slots = x_hbm.shape[2]
    pcols = x_hbm.shape[1]
    inner = HB * HD
    each_slots = slots // chips
    chip = me_ref[0] // 4
    small = [
        pltpu.make_async_copy(g1_hbm, g1_ref, sems.at[1]),
        pltpu.make_async_copy(g2_hbm, g2_ref, sems.at[2]),
        pltpu.make_async_copy(counts_hbm, counts, sems.at[0]),
    ]
    quarter = prows // 4
    loads = [
        pltpu.make_async_copy(
            x_hbm.at[pl.ds(i * quarter, quarter)], x_ref.at[pl.ds(i * quarter, quarter)], sems.at[3 + i]
        )
        for i in range(4)
    ]
    copies = []
    for i in range(3):
        cols = pl.ds(i * inner, inner)
        copies.append(pltpu.make_async_copy(w1_hbm.at[:, cols], w1.at[:, cols], wsems.at[i]))
    copies.append(pltpu.make_async_copy(w2_hbm, w2, wsems.at[3]))
    for i in range(3):
        cols = pl.ds(i * inner, inner)
        copies.append(pltpu.make_async_copy(w3_hbm.at[:, cols], w3.at[:, cols], wsems.at[4 + i]))
    small[0].start()
    for c in loads + copies[:1] + small[1:] + copies[1:3]:
        c.start()

    small[0].wait()
    g1 = g1_ref[...].astype(F32).reshape(1, width)
    for b in range(tokens // 16):
        if b % (2 * quarter) == 0:
            loads[b // (2 * quarter)].wait()
        normed[pl.ds(b * 16, 16), :] = rms(x_ref[b // pcols, b % pcols].astype(F32), g1)
    for c in copies[3:]:
        c.start()
    for i in range(3):
        copies[i].wait()
        for t in range(inner // 256):
            cols = pl.ds(i * inner + t * 256, 256)
            qkv[:, cols] = dot(normed[...], w1[:, cols]).astype(BF16)

    small[2].wait()
    block = 128
    rowi = lax.broadcasted_iota(jnp.int32, (block, block), 0)
    coli = lax.broadcasted_iota(jnp.int32, (block, block), 1)
    slot = coli % slots
    ngroups = counts.shape[0]
    cap = slots // ngroups
    count = jnp.zeros((block, block), jnp.int32)
    for g in range(ngroups):
        count = jnp.where(slot // cap == g, counts[g], count)
    mask = (rowi // slots == coli // slots) & (slot % cap < count)
    for b in range(tokens // block):
        rows = pl.ds(b * block, block)
        for t in range(HB // 2):
            q = qkv[rows, pl.ds(t * 128, 128)]
            k = qkv[rows, pl.ds(inner + t * 128, 128)]
            v = qkv[rows, pl.ds(2 * inner + t * 128, 128)]
            heads[rows, pl.ds(t * 128, 128)] = pair_attention(q, halves(k), with_ones(halves(v)), mask)

    for c in copies[3:]:
        c.wait()
    small[1].wait()
    g2 = g2_ref[...].astype(F32).reshape(1, width)
    for t in range(width // 256):
        cols = pl.ds(t * 256, 256)
        x = x_ref[:, :, :, cols].reshape(tokens, 256)
        resid_ref[:, cols] = x.astype(F32) + dot(heads[...], w2[:, cols])
    stores = [pltpu.make_async_copy(resid_ref, resid_hbm, osems.at[0])]
    stores[0].start()
    for b in range(tokens // 16):
        rows = pl.ds(b * 16, 16)
        normed[rows, :] = rms(resid_ref[rows, :], g2)

    for i in range(3):
        to = pl.ds(i * 256, 256)
        w = dot(normed[...], w3[:, pl.ds(i * inner + 256, 256)])
        wide[i % 2, 0] = w[:, :128]
        wide[i % 2, 1] = w[:, 128:]
        for d in range(chips):
            for low in range(each_slots):
                s = each_slots * (chip ^ d) + low
                for c in range(pcols):
                    part = [
                        wide[i % 2, j, pl.ds(c * slots + s, prows, stride=pcols * slots), :]
                        for j in range(2)
                    ]
                    at = pl.ds((low * pcols + c) * prows, prows)
                    col_ref[d, at, to] = jnp.concatenate(part, axis=1).astype(BF16)
    for d in range(chips):
        stores.append(pltpu.make_async_copy(col_ref.at[d], cols_hbm[d], osems.at[1 + d]))
        stores[-1].start()
    kv = pl.ds(HC * HD, 2 * HC * HD)
    stores.append(pltpu.make_async_copy(col_ref.at[0, :, kv], kv_hbm, osems.at[1 + chips]))
    stores[-1].start()
    for i in range(3):
        to = pl.ds(i * 256, 256)
        r = dot(normed[...], w3[:, pl.ds(i * inner, 256)]).astype(BF16)
        row_ref[:, :, to] = r.reshape(prows, row_flat, 256)
        stores.append(
            pltpu.make_async_copy(row_ref.at[:, :, to], row_hbm.at[:, :, to], osems.at[2 + chips + i])
        )
        stores[-1].start()
    for c in stores:
        c.wait()


def row_kernel(x_ref, o_ref, flat):
    n, each, _ = x_ref.shape
    slots = 16
    m = n * each
    block = 128
    rowi = lax.broadcasted_iota(jnp.int32, (block, m), 0)
    coli = lax.broadcasted_iota(jnp.int32, (block, m), 1)
    mask = rowi % slots == coli % slots
    x = x_ref[...].reshape(m, 3 * HR * HD)
    for t in range(HR // 2):
        k = x[:, 256 + t * 128 : 384 + t * 128]
        v = x[:, 512 + t * 128 : 640 + t * 128]
        for b in range(m // block):
            q = x[b * block : (b + 1) * block, t * 128 : (t + 1) * 128]
            flat[pl.ds(b * block, block), pl.ds(t * 128, 128)] = stacked_attention(q, k, v, mask)
    o_ref[...] = flat[...].reshape(n, each, HR * HD)


def col_kernel(*refs):
    n = 4
    pieces, others, outs = refs[:n], refs[n : 4 * n], refs[4 * n :]
    prows = 16
    each = pieces[0].shape[0]
    for g in range(each // prows):
        part = pl.ds(g * prows, prows)

        def take(refs_, at):
            return [r[part, pl.ds(at, 128)] for r in refs_]

        for t in range(HC // 2):
            at = t * 128
            k = jnp.concatenate(take(pieces, 256 + at) + take(others, at), axis=0)
            v = jnp.concatenate(take(pieces, 512 + at) + take(others, 256 + at), axis=0)
            q = jnp.concatenate(take(pieces, at), axis=0)
            o = stacked_attention(q, k, v, None)
            for d in range(n):
                outs[d][part, pl.ds(at, 128)] = o[d * prows : (d + 1) * prows]


def row_projection_kernel(resid_hbm, row_ref, w_ref, acc_ref, resid_ref, sems):
    m = acc_ref.shape[0]
    n = sems.shape[0]
    loads = []
    for i in range(n):
        rows = pl.ds(i * (m // n), m // n)
        loads.append(pltpu.make_async_copy(resid_hbm.at[rows], resid_ref.at[rows], sems.at[i]))
        loads[i].start()
    each = row_ref.shape[0] // n
    for i in range(n):
        rows = pl.ds(i * (m // n), m // n)
        x = row_ref[pl.ds(i * each, each)].reshape(m // n, row_ref.shape[2])
        loads[i].wait()
        acc_ref[rows, :] = resid_ref[rows, :] + dot(x, w_ref[...])


def column_projection_kernel(me_ref, acc_ref, p0, p1, p2, p3, w_ref, out_hbm, wide, natural, out_ref, sems):
    pieces = (p0, p1, p2, p3)
    m = acc_ref.shape[0]
    n = sems.shape[0]
    each = pieces[0].shape[0]
    slots = prows = 16
    pcols = each * len(pieces) // slots // prows
    chip = me_ref[0] // 4
    for d in range(len(pieces)):
        to = pl.ds(pl.multiple_of((chip ^ d) * each, each), each)
        for j in range(2):
            wide[j, to, :] = pieces[d][:, pl.ds(j * 128, 128)].astype(F32)
    for r in range(prows):
        for c in range(pcols):
            part = [
                wide[j, pl.ds(c * prows + r, slots, stride=pcols * prows), :] for j in range(2)
            ]
            natural[pl.ds((r * pcols + c) * slots, slots), :] = jnp.concatenate(part, axis=1).astype(BF16)
    stores = []
    for i in range(n):
        rows = pl.ds(i * (m // n), m // n)
        out_ref[rows, :] = (acc_ref[rows, :] + dot(natural[rows, :], w_ref[...])).astype(BF16)
        stores.append(pltpu.make_async_copy(out_ref.at[rows], out_hbm.at[rows], sems.at[i]))
        stores[i].start()
    for c in stores:
        c.wait()


def cost(flops, nbytes, trans=0):
    return pl.CostEstimate(flops=flops, bytes_accessed=nbytes, transcendentals=trans)


def flip(array, axes, n, by):
    return lax.ppermute(array, axes, [(i, i ^ by) for i in range(n)])


def local(tokens, counts, norm_band, w_band_qkv, w_band_out, norm_space, w_space_qkv, w_space_out):
    prows, pcols, slots, width = tokens.shape
    m = prows * pcols * slots
    inner = HB * HD
    wide = 3 * HR * HD
    xn = 4
    each = slots // xn * pcols * prows
    kv_wide = 2 * HC * HD
    rows_axes = ("band", "row")
    me = lax.axis_index(rows_axes).astype(jnp.int32).reshape(1)

    def params(mib):
        return pltpu.CompilerParams(vmem_limit_bytes=mib << 20)

    resid, row_qkv, *col_qkv, kv0 = pl.pallas_call(
        local_kernel,
        name="local",
        out_shape=(jax.ShapeDtypeStruct((m, width), F32), jax.ShapeDtypeStruct((prows, pcols * slots, wide), BF16))
        + (jax.ShapeDtypeStruct((each, wide), BF16),) * xn
        + (jax.ShapeDtypeStruct((each, kv_wide), BF16),),
        in_specs=[HBM] * 7 + [SMEM],
        out_specs=(HBM,) * (3 + xn),
        scratch_shapes=[
            pltpu.SMEM(counts.shape, jnp.int32),
            pltpu.VMEM(tokens.shape, BF16),
            pltpu.VMEM((width,), BF16),
            pltpu.VMEM((width,), BF16),
            pltpu.VMEM(w_band_qkv.shape, BF16),
            pltpu.VMEM(w_band_out.shape, BF16),
            pltpu.VMEM(w_space_qkv.shape, BF16),
            pltpu.VMEM((m, width), BF16),
            pltpu.VMEM((m, 3 * inner), BF16),
            pltpu.VMEM((m, inner), BF16),
            pltpu.VMEM((m, width), F32),
            pltpu.VMEM((prows, pcols * slots, wide), BF16),
            pltpu.VMEM((xn, each, wide), BF16),
            pltpu.VMEM((2, 2, m, 128), F32),
            pltpu.SemaphoreType.DMA((7,)),
            pltpu.SemaphoreType.DMA((7,)),
            pltpu.SemaphoreType.DMA((5 + xn,)),
        ],
        compiler_params=params(59),
        cost_estimate=cost(2 * m * width * 4096, 12 << 20),
    )(counts, tokens, norm_band, norm_space, w_band_qkv, w_band_out, w_space_qkv, me)
    row_all = lax.all_to_all(row_qkv, "col", 0, 0, tiled=True)
    pieces, kvs = [col_qkv[0]], [kv0]
    for d in range(1, xn):
        pieces.append(flip(col_qkv[d], rows_axes, slots, 4 * d))
        kvs.append(pieces[d][:, HC * HD :])
    far, core, core_far = [], [], []
    for d in range(xn):
        far.append(flip(kvs[d], rows_axes, slots, 2))
        core.append(flip(kvs[d], rows_axes, slots, 1))
        core_far.append(flip(far[d], rows_axes, slots, 1))
    row_o = pl.pallas_call(
        row_kernel,
        name="row_attention",
        out_shape=jax.ShapeDtypeStruct((prows, pcols * slots, HR * HD), BF16),
        in_specs=[VMEM], out_specs=VMEM,
        scratch_shapes=[pltpu.VMEM((m, HR * HD), BF16)],
        compiler_params=params(16),
        cost_estimate=cost(1 << 29, 1 << 20),
    )(row_all)
    row_heads = lax.all_to_all(row_o, "col", 0, 0, tiled=True)
    col_o = pl.pallas_call(
        col_kernel,
        name="column_attention",
        out_shape=(jax.ShapeDtypeStruct((each, HC * HD), BF16),) * xn,
        in_specs=[VMEM] * (4 * xn),
        out_specs=(VMEM,) * xn,
        compiler_params=params(16),
        cost_estimate=cost(1 << 28, 1 << 20),
    )(*pieces, *far, *core, *core_far)
    back = [col_o[0]]
    for d in range(1, xn):
        back.append(flip(col_o[d], rows_axes, slots, 4 * d))
    acc = pl.pallas_call(
        row_projection_kernel,
        name="row_projection",
        out_shape=jax.ShapeDtypeStruct((m, width), F32),
        in_specs=[HBM, VMEM, VMEM], out_specs=VMEM,
        scratch_shapes=[pltpu.VMEM((m, width), F32), pltpu.SemaphoreType.DMA((4,))],
        compiler_params=params(50),
        cost_estimate=cost(2 * m * width * 256, 5 << 20),
    )(resid, row_heads, w_space_out[: HR * HD])
    out = pl.pallas_call(
        column_projection_kernel,
        name="column_projection",
        out_shape=jax.ShapeDtypeStruct((m, width), BF16),
        in_specs=[SMEM] + [VMEM] * (xn + 2), out_specs=HBM,
        scratch_shapes=[
            pltpu.VMEM((2, m, 128), F32),
            pltpu.VMEM((m, HC * HD), BF16),
            pltpu.VMEM((m, width), BF16),
            pltpu.SemaphoreType.DMA((4,)),
        ],
        compiler_params=params(16),
        cost_estimate=cost(2 * m * width * 256, 5 << 20),
    )(me, acc, *back, w_space_out[HR * HD :])
    return out.reshape(prows, pcols, slots, width)


def solution(mesh):
    placed = (P(("band", "row"), "col", None, None), P(), P(), P(), P(), P(), P(), P())
    return jax.shard_map(
        local,
        mesh=mesh,
        in_specs=placed,
        out_specs=P(("band", "row"), "col", None, None),
        check_vma=False,
    )
```
